32 devices in a mesh: tm: 8 (over z, y), space: 4 (over x, core).
Axes of the slice: x: 2, y: 2, z: 4, core: 2. Of those that a mesh axis runs over, the one named last changes fastest.
Arguments:
- video_in: bfloat16 [8, 256, 64, 128], P('tm', 'space'), may hold values from -6 to 6
- cotangent: bfloat16 [8, 256, 64, 128], P('tm', 'space'), may hold values from -6 to 6
- kernel_a: bfloat16 [3, 3, 3, 64, 64], replicated, may hold values from -0.15625 to 0.15625
- kernel_b: bfloat16 [3, 3, 3, 64, 64], replicated, may hold values from -0.15625 to 0.15625
- plane_kernel: bfloat16 [3, 3, 64, 64], replicated, may hold values from -0.25 to 0.25
- plane_head: bfloat16 [64], replicated, may hold values from -0.75 to 0.75
- time_kernel: bfloat16 [3, 64, 64], replicated, may hold values from -0.4375 to 0.4375
- time_mixer: bfloat16 [64, 64], replicated, may hold values from -12 to 12
- time_head: bfloat16 [64], replicated, may hold values from -0.75 to 0.75
- listed: int32 [8], replicated, may hold values from 0 to 7, as said below
Outputs:
- video: bfloat16 [8, 256, 64, 128], P('tm', 'space')
- input_grad: bfloat16 [8, 256, 64, 128], P('tm', 'space')
- plane_scores: float32 [8, 4, 64, 128], P('tm', 'space')
- time_scores: float32 [4, 32, 64], P('space', 'tm')
The draws below stay inside these ranges and needn't reach their ends.
Inputs may be any that keep to these rules, and one draw needn't show every extreme that they name: `listed`: 8 distinct frame indices; the first is always frame 8 // 2, and frames 0 and 7 are always among the others, which stand in random order.
All inputs are finite; a program needn't handle non-finite values.
Results may differ from the reference program's by a relative error of at most 0.0053.
Values may be sent and summed in bfloat16 or wider, within the bound.
A program may use at most 128 MiB of HBM per device.

```python
import jax
import jax.numpy as jnp
from jax import lax

C = 64
RD = 64
W = 128
LISTED = 8
NT = 8
H = 256
HPT = 32
WP = 64
N_TM = 8
N_SPACE = 4


def draw_listed(key, part):
    half_frame = NT // 2
    drawn = 1 + jax.random.permutation(jax.random.fold_in(key, 11), NT - 3)[:LISTED - 3]
    drawn = drawn.astype(jnp.int32)
    middle = jnp.where(drawn >= half_frame, drawn + 1, drawn)
    others = jnp.concatenate([jnp.array([0, NT - 1], jnp.int32), middle])
    shuffle = jax.random.permutation(jax.random.fold_in(key, 12), LISTED - 1)
    return jnp.concatenate([jnp.array([half_frame], jnp.int32), others[shuffle]])


def block_scale(own_key, shape, shards, low, top_value):
    factor_of, own = 1.0, jax.random.fold_in(own_key, 6)
    for position, parts in shards:
        steps = jnp.exp(jax.random.uniform(jax.random.fold_in(own, position), (parts,), jnp.float32, low / len(shards), top_value / len(shards)))
        factor_of = factor_of * jnp.repeat(steps, shape[position] // parts).reshape([-1 if axis == position else 1 for axis in range(len(shape))])
    return factor_of


def gaussian(stream_key, shape, spread, most, cuts=(), dtype=jnp.bfloat16):
    values = spread * jax.random.normal(stream_key, shape, jnp.float32)
    if cuts:
        values = values * block_scale(stream_key, shape, cuts, -0.22, 0.18)
    return jnp.clip(values, -most, most).astype(dtype)


def setup_inputs(seed: int = 0) -> dict:
    key_list = jax.random.split(jax.random.key(seed), 11)
    video_in = gaussian(key_list[0], (NT, H, C, W), 1.0, 6.0, ((0, 8), (1, 4)))
    cotangent = gaussian(key_list[1], (NT, H, C, W), 1.0, 6.0, ((0, 8), (1, 4)))
    kernel_a = gaussian(key_list[2], (3, 3, 3, C, C), (27 * C) ** -0.5, 0.15625)
    kernel_b = gaussian(key_list[3], (3, 3, 3, C, C), (27 * C) ** -0.5, 0.15625)
    plane_kernel = gaussian(key_list[4], (3, 3, C, C), (9 * C) ** -0.5, 0.25)
    plane_head = gaussian(key_list[5], (C,), C ** -0.5, 0.75)
    time_kernel = gaussian(key_list[6], (3, C, C), (3 * C) ** -0.5, 0.4375)
    time_mixer = gaussian(key_list[7], (C, C), (C ** -0.5 * 16), 12.0)
    time_head = gaussian(key_list[8], (C,), C ** -0.5, 0.75)
    listed = draw_listed(jax.random.fold_in(key_list[10], 71), 0)
    return {"video_in": video_in, "cotangent": cotangent, "kernel_a": kernel_a, "kernel_b": kernel_b, "plane_kernel": plane_kernel, "plane_head": plane_head, "time_kernel": time_kernel, "time_mixer": time_mixer, "time_head": time_head, "listed": listed}


def cube_conv(volume, kernel):
    padded = jnp.pad(volume.astype(jnp.float32), ((1, 1), (1, 1), (0, 0), (0, 0)))
    return lax.conv_general_dilated(padded[None], kernel.astype(jnp.float32), (1, 1, 1), [(0, 0), (0, 0), (1, 1)], dimension_numbers=("NDHCW", "DHWIO", "NDHCW"), precision=lax.Precision.HIGHEST)[0]


def flipped(kernel):
    return jnp.swapaxes(kernel[::-1, ::-1, ::-1], 3, 4)


def silu_slope(values):
    logistic = jax.nn.sigmoid(values)
    return logistic * (1.0 + values * (1.0 - logistic))


def plane_map(frames, kernel, head):
    padded = jnp.pad(frames.astype(jnp.float32), ((0, 0), (1, 1), (0, 0), (0, 0)))
    conv_out = lax.conv_general_dilated(padded, kernel.astype(jnp.float32), (1, 1), [(0, 0), (1, 1)], dimension_numbers=("NHCW", "HWIO", "NHCW"), precision=lax.Precision.HIGHEST)
    return jnp.einsum("nhow,o->nhw", jax.nn.silu(conv_out), head.astype(jnp.float32), precision=lax.Precision.HIGHEST)


def pool_pairs(volume):
    shaped = volume.astype(jnp.float32).reshape(volume.shape[0], volume.shape[1] // 2, 2, volume.shape[2], volume.shape[3] // 2, 2)
    return jnp.mean(shaped, axis=(2, 5)).astype(jnp.bfloat16)


def time_conv(rimmed, kernel):
    length = rimmed.shape[0] - 2
    total = jnp.zeros((length, rimmed.shape[1], kernel.shape[2], rimmed.shape[3]), jnp.float32)
    for offset in range(3):
        total = total + jnp.einsum("thcw,co->thow", rimmed[offset:offset + length].astype(jnp.float32), kernel[offset].astype(jnp.float32), precision=lax.Precision.HIGHEST)
    return total


def time_head_map(time_mean, mixer, head):
    mixed_units = jnp.einsum("hcw,co->how", time_mean, mixer.astype(jnp.float32), precision=lax.Precision.HIGHEST)
    return jnp.einsum("how,o->hw", jax.nn.silu(mixed_units), head.astype(jnp.float32), precision=lax.Precision.HIGHEST)


def reference(video_in, cotangent, kernel_a, kernel_b, plane_kernel, plane_head, time_kernel, time_mixer, time_head, listed):
    float_in = video_in.astype(jnp.float32)
    hidden_in = jax.nn.silu(float_in).astype(jnp.bfloat16)
    pre_act = cube_conv(hidden_in, kernel_a)
    inner_act = jax.nn.silu(pre_act).astype(jnp.bfloat16)
    generated = (float_in + cube_conv(inner_act, kernel_b)).astype(jnp.bfloat16)
    grad_pre = (cube_conv(cotangent, flipped(kernel_b)) * silu_slope(pre_act)).astype(jnp.bfloat16)
    input_grad = (cotangent.astype(jnp.float32) + cube_conv(grad_pre, flipped(kernel_a)) * silu_slope(float_in)).astype(jnp.bfloat16)
    chosen = jnp.take(generated, listed, axis=0)
    plane_all = plane_map(chosen, plane_kernel, plane_head)
    groups = N_TM // LISTED
    quarter = RD // groups
    plane_scores = plane_all.reshape(LISTED, N_SPACE, groups, quarter, W).transpose(0, 2, 1, 3, 4).reshape(N_TM, N_SPACE, quarter, W)
    pooled = pool_pairs(generated)
    rimmed = jnp.pad(pooled, ((1, 1), (0, 0), (0, 0), (0, 0)))
    time_mean = jnp.mean(jax.nn.silu(time_conv(rimmed, time_kernel)), axis=0)
    time_scores = time_head_map(time_mean, time_mixer, time_head).reshape(N_SPACE, HPT, WP)
    return generated, input_grad, plane_scores, time_scores
```

```python
import functools

import jax
import jax.numpy as jnp
from jax import lax
from jax.experimental import pallas as pl
from jax.experimental.pallas import tpu as pltpu
from jax.sharding import PartitionSpec as P


LISTED = 8
F32 = jnp.float32
BF16 = jnp.bfloat16


def logistic(values):
    return 1.0 / (1.0 + jnp.exp(-values))


def slope_of(values):
    s = logistic(values)
    return s * (1.0 + values * (1.0 - s))


def store_shifted(wide_ref, t, row, values):
    channels, width = values.shape
    lane = lax.broadcasted_iota(jnp.int32, values.shape, 1)
    before = jnp.where(lane == 0, 0.0, pltpu.roll(values, 1, 1))
    after = jnp.where(lane == width - 1, 0.0, pltpu.roll(values, width - 1, 1))
    wide_ref[t, row, 0:channels] = before.astype(BF16)
    wide_ref[t, row, channels : 2 * channels] = values.astype(BF16)
    wide_ref[t, row, 2 * channels : 3 * channels] = after.astype(BF16)


def fill(wide_ref, main_ref, top_ref, bottom_ref, change):
    frames, rows = main_ref.shape[:2]

    def per_frame(t, _):
        store_shifted(wide_ref, t, 0, change(top_ref[t, 0].astype(F32)))
        store_shifted(wide_ref, t, rows + 1, change(bottom_ref[t, 0].astype(F32)))
        for row in range(rows):
            store_shifted(wide_ref, t, row + 1, change(main_ref[t, row].astype(F32)))
        return 0

    lax.fori_loop(0, frames, per_frame, 0)


def slab(wide_ref, t, row):
    depth = 3 * wide_ref.shape[2]
    width = wide_ref.shape[3]
    left = wide_ref[t, pl.ds(row, 3)].reshape(depth, width)
    right = wide_ref[t, pl.ds(row + 1, 3)].reshape(depth, width)
    return jnp.concatenate([left, right], axis=1)


def conv_loop(wide_ref, weight_ref, rows, emit):
    frames = wide_ref.shape[0]
    out = weight_ref.shape[0] // 3

    def product(t, row):
        return jnp.dot(weight_ref[...], slab(wide_ref, t, row), preferred_element_type=F32)

    def pair(i, _):
        row = 2 * i
        first = product(0, row)

        def step(t, carry):
            ready, early = carry
            z = product(t, row)
            emit(t - 1, row, ready + z[2 * out :])
            return early + z[out : 2 * out], z[:out]

        carry = (first[out : 2 * out], first[:out])
        if frames <= 8:
            for t in range(1, frames):
                carry = step(t, carry)
        else:
            carry = lax.fori_loop(1, frames, step, carry)
        emit(frames - 1, row, carry[0])
        return 0

    lax.fori_loop(0, rows // 2, pair, 0)


def each_row(emit_row, width):
    def emit(t, row, total):
        emit_row(t, row, total[:, :width])
        emit_row(t, row + 1, total[:, width:])

    return emit


def edges(out_ref, first_ref, last_ref):
    rows = out_ref.shape[1]
    first_ref[...] = out_ref[:, 0:1]
    last_ref[...] = out_ref[:, rows - 1 : rows]


def pre_kernel(main_ref, top_ref, bottom_ref, weight_ref, inner_ref, slope_ref, first_ref, last_ref, wide_ref):
    rows, width = main_ref.shape[1], main_ref.shape[3]
    fill(wide_ref, main_ref, top_ref, bottom_ref, lambda v: v * logistic(v))

    def emit(t, row, total):
        s = logistic(total)
        inner_ref[t, row] = (total * s).astype(BF16)
        slope_ref[t, row] = s * (1.0 + total * (1.0 - s))

    conv_loop(wide_ref, weight_ref, rows, each_row(emit, width))
    edges(inner_ref, first_ref, last_ref)


def grad_pre_kernel(main_ref, top_ref, bottom_ref, weight_ref, slope_ref, out_ref, first_ref, last_ref, wide_ref):
    rows, width = main_ref.shape[1], main_ref.shape[3]
    fill(wide_ref, main_ref, top_ref, bottom_ref, lambda v: v)

    def emit(t, row, total):
        out_ref[t, row] = (total * slope_ref[t, row]).astype(BF16)

    conv_loop(wide_ref, weight_ref, rows, each_row(emit, width))
    edges(out_ref, first_ref, last_ref)


def video_kernel(main_ref, top_ref, bottom_ref, weight_ref, in_ref, out_ref, first_ref, last_ref, wide_ref):
    rows, width = main_ref.shape[1], main_ref.shape[3]
    fill(wide_ref, main_ref, top_ref, bottom_ref, lambda v: v)

    def emit(t, row, total):
        out_ref[t, row] = (in_ref[t, row].astype(F32) + total).astype(BF16)

    conv_loop(wide_ref, weight_ref, rows, each_row(emit, width))
    edges(out_ref, first_ref, last_ref)


def input_grad_kernel(main_ref, top_ref, bottom_ref, weight_ref, in_ref, cot_ref, out_ref, wide_ref):
    rows, width = main_ref.shape[1], main_ref.shape[3]
    fill(wide_ref, main_ref, top_ref, bottom_ref, lambda v: v)

    def emit(t, row, total):
        gain = slope_of(in_ref[t, row].astype(F32))
        out_ref[t, row] = (cot_ref[t, row].astype(F32) + total * gain).astype(BF16)

    conv_loop(wide_ref, weight_ref, rows, each_row(emit, width))


def score_kernel(
    listed_ref,
    main_ref,
    top_ref,
    bottom_ref,
    plane_ref,
    plane_head_ref,
    pool_ref,
    time_ref,
    mixer_ref,
    time_head_ref,
    plane_out_ref,
    time_out_ref,
    wide_ref,
    pooled_ref,
):
    frames, rows, channels, width = main_ref.shape
    half = width // 2

    def per_listed(k, _):
        t = listed_ref[k]
        store_shifted(wide_ref, 0, 0, top_ref[t, 0].astype(F32))
        store_shifted(wide_ref, 0, rows + 1, bottom_ref[t, 0].astype(F32))
        for row in range(rows):
            store_shifted(wide_ref, 0, row + 1, main_ref[t, row].astype(F32))
        for row in range(0, rows, 2):
            g = jnp.dot(plane_ref[...], slab(wide_ref, 0, row), preferred_element_type=F32)
            scores = jnp.sum(g * logistic(g) * plane_head_ref[...], axis=0, keepdims=True)
            plane_out_ref[k, row : row + 1] = scores[:, :width]
            plane_out_ref[k, row + 1 : row + 2] = scores[:, width:]
        return 0

    lax.fori_loop(0, plane_out_ref.shape[0], per_listed, 0)

    def per_row(i, _):
        zero = jnp.zeros((channels, half), BF16)
        pooled_ref[0:channels] = zero
        pooled_ref[(frames + 1) * channels :] = zero
        for t in range(frames):
            both = jnp.concatenate([main_ref[t, 2 * i], main_ref[t, 2 * i + 1]], axis=1)
            mean = jnp.dot(both, pool_ref[...], preferred_element_type=F32)
            pooled_ref[(t + 1) * channels : (t + 2) * channels] = mean.astype(BF16)
        total = jnp.zeros((time_ref.shape[0], half), F32)
        for t in range(frames):
            q = jnp.dot(
                time_ref[...],
                pooled_ref[t * channels : (t + 3) * channels],
                preferred_element_type=F32,
            )
            total = total + q * logistic(q)
        mixed = jnp.dot(
            mixer_ref[...],
            total / frames,
            precision=lax.Precision.HIGHEST,
            preferred_element_type=F32,
        )
        time_out_ref[i] = jnp.sum(
            mixed * logistic(mixed) * time_head_ref[...], axis=0, keepdims=True
        )
        return 0

    lax.fori_loop(0, rows // 2, per_row, 0)


def call(kernel, outs, scratch, smem, *operands):
    return run(kernel, outs, scratch, smem, operands)


def run(kernel, outs, scratch, smem, operands):
    vmem = pl.BlockSpec(memory_space=pltpu.VMEM)
    specs = [pl.BlockSpec(memory_space=pltpu.SMEM)] * smem + [vmem] * (len(operands) - smem)
    return pl.pallas_call(
        kernel,
        out_shape=[jax.ShapeDtypeStruct(shape, dtype) for shape, dtype in outs],
        in_specs=specs,
        out_specs=[vmem] * len(outs),
        scratch_shapes=[pltpu.VMEM(shape, dtype) for shape, dtype in scratch],
        compiler_params=pltpu.CompilerParams(vmem_limit_bytes=56 * 1024 * 1024),
    )(*operands)


def forward_weight(kernel):
    a, b, e, c, o = kernel.shape
    return kernel.transpose(0, 4, 1, 2, 3).reshape(a * o, b * e * c)


def backward_weight(kernel):
    a, b, e, o, c = kernel.shape
    return kernel[::-1, ::-1, ::-1].transpose(0, 3, 1, 2, 4).reshape(a * o, b * e * c)


def from_neighbours(first, last):
    tiles, parts = lax.axis_size("space"), lax.axis_size("tm")
    order = [part * tiles + tile for tile in range(tiles) for part in range(parts)]
    up = list(zip(order[:-1], order[1:]))
    down = [(j, i) for i, j in up]
    names = ("tm", "space")
    return lax.ppermute(last, names, up), lax.ppermute(first, names, down)


def shards(
    video_in,
    cotangent,
    kernel_a,
    kernel_b,
    plane_kernel,
    plane_head,
    time_kernel,
    time_mixer,
    time_head,
    listed,
):
    to_rows = functools.partial(lax.all_to_all, axis_name="tm", split_axis=1, concat_axis=0, tiled=True)
    to_frames = functools.partial(lax.all_to_all, axis_name="tm", split_axis=0, concat_axis=1, tiled=True)
    tm_count = lax.axis_size("tm")

    v = to_rows(video_in)
    frames, rows, channels, width = v.shape
    v_halo = from_neighbours(v[:, :1], v[:, rows - 1 :])
    cot = to_rows(cotangent)
    cot_halo = from_neighbours(cot[:, :1], cot[:, rows - 1 :])

    block = (v.shape, BF16)
    edge = ((frames, 1, channels, width), BF16)
    wide = ((frames, rows + 2, 3 * channels, width), BF16)

    inner, slope, first, last = call(
        pre_kernel, [block, (v.shape, F32), edge, edge], [wide], 0, v, *v_halo, forward_weight(kernel_a)
    )
    inner_halo = from_neighbours(first, last)
    grad_pre, first, last = call(
        grad_pre_kernel, [block, edge, edge], [wide], 0, cot, *cot_halo, backward_weight(kernel_b), slope
    )
    grad_halo = from_neighbours(first, last)
    video_rows, first, last = call(
        video_kernel, [block, edge, edge], [wide], 0, inner, *inner_halo, forward_weight(kernel_b), v
    )
    video_halo = from_neighbours(first, last)
    video = to_frames(video_rows)
    (grad_rows,) = call(input_grad_kernel, [block], [wide], 0, grad_pre, *grad_halo, backward_weight(kernel_a), v, cot)
    input_grad = to_frames(grad_rows)

    column = jnp.arange(width, dtype=jnp.int32) // 2
    pool = (column[:, None] == jnp.arange(width // 2, dtype=jnp.int32)[None, :]).astype(BF16) * 0.25
    pool = jnp.concatenate([pool, pool], axis=0).astype(BF16)
    b, e, c, o = plane_kernel.shape
    plane_weight = plane_kernel.reshape(b * e * c, o).T
    time_weight = time_kernel.reshape(-1, time_kernel.shape[2]).T
    maps, time_scores = call(
        score_kernel,
        [((LISTED, rows, width), F32), ((rows // 2, 1, width // 2), F32)],
        [
            ((1, rows + 2, 3 * channels, width), BF16),
            (((frames + 2) * channels, width // 2), BF16),
        ],
        1,
        listed,
        video_rows,
        *video_halo,
        plane_weight,
        plane_head.astype(F32)[:, None],
        pool,
        time_weight,
        time_mixer.astype(F32).T,
        time_head.astype(F32)[:, None],
    )
    groups = tm_count // LISTED
    moved = lax.all_to_all(jnp.repeat(maps, groups, axis=0), "tm", split_axis=0, concat_axis=0, tiled=True)
    moved = moved.reshape(groups, tm_count * rows // groups, width)
    if groups > 1:
        mine = lax.rem(lax.axis_index("tm"), groups)
        moved = lax.dynamic_index_in_dim(moved, mine, 0, keepdims=True)
    plane_scores = moved[:, None]
    return (video, input_grad, plane_scores, time_scores.reshape(1, rows // 2, width // 2))


def solution(mesh):
    return jax.shard_map(
        shards,
        mesh=mesh,
        in_specs=(
            P("tm", "space", None, None),
            P("tm", "space", None, None),
            P(),
            P(),
            P(),
            P(),
            P(),
            P(),
            P(),
            P(),
        ),
        out_specs=(
            P("tm", "space", None, None),
            P("tm", "space", None, None),
            P("tm", "space", None, None),
            P("space", "tm", None),
        ),
        check_vma=False,
    )
```

```python
import functools

import jax
import jax.numpy as jnp
from jax import lax
from jax.experimental import pallas as pl
from jax.experimental.pallas import tpu as pltpu
from jax.sharding import PartitionSpec as P


LISTED = 8
F32 = jnp.float32
BF16 = jnp.bfloat16


def logistic(values):
    return 1.0 / (1.0 + jnp.exp(-values))


def slope_of(values):
    s = logistic(values)
    return s * (1.0 + values * (1.0 - s))


def store_shifted(wide_ref, t, row, values):
    channels, width = values.shape
    lane = lax.broadcasted_iota(jnp.int32, values.shape, 1)
    before = jnp.where(lane == 0, 0.0, pltpu.roll(values, 1, 1))
    after = jnp.where(lane == width - 1, 0.0, pltpu.roll(values, width - 1, 1))
    wide_ref[t, row, 0:channels] = before.astype(BF16)
    wide_ref[t, row, channels : 2 * channels] = values.astype(BF16)
    wide_ref[t, row, 2 * channels : 3 * channels] = after.astype(BF16)


def fill(wide_ref, main_ref, top_ref, bottom_ref, change):
    frames, rows = main_ref.shape[:2]

    def per_frame(t, _):
        store_shifted(wide_ref, t, 0, change(top_ref[t, 0].astype(F32)))
        store_shifted(wide_ref, t, rows + 1, change(bottom_ref[t, 0].astype(F32)))
        for row in range(rows):
            store_shifted(wide_ref, t, row + 1, change(main_ref[t, row].astype(F32)))
        return 0

    lax.fori_loop(0, frames, per_frame, 0)


def slab(wide_ref, t, row):
    depth = 3 * wide_ref.shape[2]
    width = wide_ref.shape[3]
    left = wide_ref[t, pl.ds(row, 3)].reshape(depth, width)
    right = wide_ref[t, pl.ds(row + 1, 3)].reshape(depth, width)
    return jnp.concatenate([left, right], axis=1)


def conv_loop(wide_ref, weight_ref, rows, emit):
    frames = wide_ref.shape[0]
    out = weight_ref.shape[0] // 3

    def product(t, row):
        return jnp.dot(weight_ref[...], slab(wide_ref, t, row), preferred_element_type=F32)

    def pair(i, _):
        row = 2 * i
        first = product(0, row)

        def step(t, carry):
            ready, early = carry
            z = product(t, row)
            emit(t - 1, row, ready + z[2 * out :])
            return early + z[out : 2 * out], z[:out]

        carry = (first[out : 2 * out], first[:out])
        if frames <= 8:
            for t in range(1, frames):
                carry = step(t, carry)
        else:
            carry = lax.fori_loop(1, frames, step, carry)
        emit(frames - 1, row, carry[0])
        return 0

    lax.fori_loop(0, rows // 2, pair, 0)


def each_row(emit_row, width):
    def emit(t, row, total):
        emit_row(t, row, total[:, :width])
        emit_row(t, row + 1, total[:, width:])

    return emit


def edges(out_ref, first_ref, last_ref):
    rows = out_ref.shape[1]
    first_ref[...] = out_ref[:, 0:1]
    last_ref[...] = out_ref[:, rows - 1 : rows]


def pre_kernel(main_ref, top_ref, bottom_ref, weight_ref, inner_ref, slope_ref, first_ref, last_ref, wide_ref):
    rows, width = main_ref.shape[1], main_ref.shape[3]
    fill(wide_ref, main_ref, top_ref, bottom_ref, lambda v: v * logistic(v))

    def emit(t, row, total):
        s = logistic(total)
        inner_ref[t, row] = (total * s).astype(BF16)
        slope_ref[t, row] = s * (1.0 + total * (1.0 - s))

    conv_loop(wide_ref, weight_ref, rows, each_row(emit, width))
    edges(inner_ref, first_ref, last_ref)


def grad_pre_kernel(main_ref, top_ref, bottom_ref, weight_ref, slope_ref, out_ref, first_ref, last_ref, wide_ref):
    rows, width = main_ref.shape[1], main_ref.shape[3]
    fill(wide_ref, main_ref, top_ref, bottom_ref, lambda v: v)

    def emit(t, row, total):
        out_ref[t, row] = (total * slope_ref[t, row]).astype(BF16)

    conv_loop(wide_ref, weight_ref, rows, each_row(emit, width))
    edges(out_ref, first_ref, last_ref)


def video_kernel(main_ref, top_ref, bottom_ref, weight_ref, in_ref, out_ref, first_ref, last_ref, wide_ref):
    rows, width = main_ref.shape[1], main_ref.shape[3]
    fill(wide_ref, main_ref, top_ref, bottom_ref, lambda v: v)

    def emit(t, row, total):
        out_ref[t, row] = (in_ref[t, row].astype(F32) + total).astype(BF16)

    conv_loop(wide_ref, weight_ref, rows, each_row(emit, width))
    edges(out_ref, first_ref, last_ref)


def input_grad_kernel(main_ref, top_ref, bottom_ref, weight_ref, in_ref, cot_ref, out_ref, wide_ref):
    rows, width = main_ref.shape[1], main_ref.shape[3]
    fill(wide_ref, main_ref, top_ref, bottom_ref, lambda v: v)

    def emit(t, row, total):
        gain = slope_of(in_ref[t, row].astype(F32))
        out_ref[t, row] = (cot_ref[t, row].astype(F32) + total * gain).astype(BF16)

    conv_loop(wide_ref, weight_ref, rows, each_row(emit, width))


def score_kernel(
    listed_ref,
    main_ref,
    top_ref,
    bottom_ref,
    plane_ref,
    plane_head_ref,
    pool_ref,
    time_ref,
    mixer_ref,
    time_head_ref,
    plane_out_ref,
    time_out_ref,
    wide_ref,
    pooled_ref,
):
    frames, rows, channels, width = main_ref.shape
    half = width // 2

    def per_listed(k, _):
        t = listed_ref[k]
        store_shifted(wide_ref, 0, 0, top_ref[t, 0].astype(F32))
        store_shifted(wide_ref, 0, rows + 1, bottom_ref[t, 0].astype(F32))
        for row in range(rows):
            store_shifted(wide_ref, 0, row + 1, main_ref[t, row].astype(F32))
        for row in range(0, rows, 2):
            g = jnp.dot(plane_ref[...], slab(wide_ref, 0, row), preferred_element_type=F32)
            scores = jnp.sum(g * logistic(g) * plane_head_ref[...], axis=0, keepdims=True)
            plane_out_ref[k, row : row + 1] = scores[:, :width]
            plane_out_ref[k, row + 1 : row + 2] = scores[:, width:]
        return 0

    lax.fori_loop(0, plane_out_ref.shape[0], per_listed, 0)

    def per_row(i, _):
        zero = jnp.zeros((channels, half), BF16)
        pooled_ref[0:channels] = zero
        pooled_ref[(frames + 1) * channels :] = zero
        for t in range(frames):
            both = jnp.concatenate([main_ref[t, 2 * i], main_ref[t, 2 * i + 1]], axis=1)
            mean = jnp.dot(both, pool_ref[...], preferred_element_type=F32)
            pooled_ref[(t + 1) * channels : (t + 2) * channels] = mean.astype(BF16)
        total = jnp.zeros((time_ref.shape[0], half), F32)
        for t in range(frames):
            q = jnp.dot(
                time_ref[...],
                pooled_ref[t * channels : (t + 3) * channels],
                preferred_element_type=F32,
            )
            total = total + q * logistic(q)
        mixed = jnp.dot(
            mixer_ref[...],
            total / frames,
            precision=lax.Precision.HIGHEST,
            preferred_element_type=F32,
        )
        time_out_ref[i] = jnp.sum(
            mixed * logistic(mixed) * time_head_ref[...], axis=0, keepdims=True
        )
        return 0

    lax.fori_loop(0, rows // 2, per_row, 0)


def call(kernel, outs, scratch, smem, *operands):
    return run(kernel, outs, scratch, smem, operands)


def run(kernel, outs, scratch, smem, operands):
    vmem = pl.BlockSpec(memory_space=pltpu.VMEM)
    specs = [pl.BlockSpec(memory_space=pltpu.SMEM)] * smem + [vmem] * (len(operands) - smem)
    return pl.pallas_call(
        kernel,
        out_shape=[jax.ShapeDtypeStruct(shape, dtype) for shape, dtype in outs],
        in_specs=specs,
        out_specs=[vmem] * len(outs),
        scratch_shapes=[pltpu.VMEM(shape, dtype) for shape, dtype in scratch],
        compiler_params=pltpu.CompilerParams(vmem_limit_bytes=56 * 1024 * 1024),
    )(*operands)


def forward_weight(kernel):
    a, b, e, c, o = kernel.shape
    return kernel.transpose(0, 4, 1, 2, 3).reshape(a * o, b * e * c)


def backward_weight(kernel):
    a, b, e, o, c = kernel.shape
    return kernel[::-1, ::-1, ::-1].transpose(0, 3, 1, 2, 4).reshape(a * o, b * e * c)


def halo_kernel(first_ref, last_ref, top_ref, bottom_ref, send_sem, recv_sem):
    parts, tiles = lax.axis_size("tm"), lax.axis_size("space")
    place = lax.axis_index("space") * parts + lax.axis_index("tm")
    has_before, has_after = place > 0, place < parts * tiles - 1
    lower, upper = jnp.maximum(place - 1, 0), jnp.minimum(place + 1, parts * tiles - 1)
    before = (lax.rem(lower, parts), lower // parts)
    after = (lax.rem(upper, parts), upper // parts)

    def move(source, target, slot, device):
        return pltpu.make_async_remote_copy(
            src_ref=source,
            dst_ref=target,
            send_sem=send_sem.at[slot],
            recv_sem=recv_sem.at[slot],
            device_id=device,
            device_id_type=pl.DeviceIdType.MESH,
        )

    def down():
        return move(first_ref, bottom_ref, 0, before)

    def up():
        return move(last_ref, top_ref, 1, after)

    barrier = pltpu.get_barrier_semaphore()

    @pl.when(has_before)
    def _():
        pl.semaphore_signal(barrier, inc=1, device_id=before, device_id_type=pl.DeviceIdType.MESH)

    @pl.when(has_after)
    def _():
        pl.semaphore_signal(barrier, inc=1, device_id=after, device_id_type=pl.DeviceIdType.MESH)

    pl.semaphore_wait(barrier, has_before.astype(jnp.int32) + has_after.astype(jnp.int32))

    @pl.when(has_before)
    def _():
        down().start()

    @pl.when(has_after)
    def _():
        up().start()

    @pl.when(jnp.logical_not(has_before))
    def _():
        top_ref[...] = jnp.zeros(top_ref.shape, top_ref.dtype)

    @pl.when(jnp.logical_not(has_after))
    def _():
        bottom_ref[...] = jnp.zeros(bottom_ref.shape, bottom_ref.dtype)

    @pl.when(has_before)
    def _():
        down().wait_send()
        up().wait_recv()

    @pl.when(has_after)
    def _():
        up().wait_send()
        down().wait_recv()


def from_neighbours(first, last, number):
    vmem = pl.BlockSpec(memory_space=pltpu.VMEM)
    edge = jax.ShapeDtypeStruct(first.shape, first.dtype)
    return pl.pallas_call(
        halo_kernel,
        name="halo",
        out_shape=[edge, edge],
        in_specs=[vmem] * 2,
        out_specs=[vmem] * 2,
        scratch_shapes=[pltpu.SemaphoreType.DMA((2,)), pltpu.SemaphoreType.DMA((2,))],
        compiler_params=pltpu.CompilerParams(collective_id=number, has_side_effects=True),
    )(first, last)


def swap_kernel(groups, in_ref, out_ref, local_sem, send_sem, recv_sem):
    parts = lax.axis_size("tm")
    me, tile = lax.axis_index("tm"), lax.axis_index("space")
    barrier = pltpu.get_barrier_semaphore()
    for d in range(1, parts):
        pl.semaphore_signal(
            barrier,
            inc=1,
            device_id=(lax.rem(me + d, parts), tile),
            device_id_type=pl.DeviceIdType.MESH,
        )
    pl.semaphore_wait(barrier, parts - 1)
    copies = []
    for d in range(1, parts):
        peer = lax.rem(me + d, parts)
        copies.append(
            pltpu.make_async_remote_copy(
                src_ref=in_ref.at[peer // groups],
                dst_ref=out_ref.at[me],
                send_sem=send_sem.at[d],
                recv_sem=recv_sem.at[d],
                device_id=(peer, tile),
                device_id_type=pl.DeviceIdType.MESH,
            )
        )
    for copy in copies:
        copy.start()
    own = pltpu.make_async_copy(in_ref.at[me // groups], out_ref.at[me], local_sem)
    own.start()
    own.wait()
    for copy in copies:
        copy.wait()


def swap(array, number):
    parts = lax.axis_size("tm")
    anywhere = pl.BlockSpec(memory_space=pl.ANY)
    return pl.pallas_call(
        functools.partial(swap_kernel, parts // array.shape[0]),
        name="swap",
        out_shape=jax.ShapeDtypeStruct((parts,) + array.shape[1:], array.dtype),
        in_specs=[anywhere],
        out_specs=anywhere,
        scratch_shapes=[
            pltpu.SemaphoreType.DMA,
            pltpu.SemaphoreType.DMA((parts,)),
            pltpu.SemaphoreType.DMA((parts,)),
        ],
        compiler_params=pltpu.CompilerParams(collective_id=number, has_side_effects=True),
    )(array)


def shards(
    video_in,
    cotangent,
    kernel_a,
    kernel_b,
    plane_kernel,
    plane_head,
    time_kernel,
    time_mixer,
    time_head,
    listed,
):
    to_rows = functools.partial(lax.all_to_all, axis_name="tm", split_axis=1, concat_axis=0, tiled=True)
    to_frames = functools.partial(lax.all_to_all, axis_name="tm", split_axis=0, concat_axis=1, tiled=True)
    tm_count = lax.axis_size("tm")

    here, height, channels, width = video_in.shape
    rows = height // tm_count
    v = swap(video_in.reshape(tm_count, rows, channels, width), 0)
    cotangent, v = lax.optimization_barrier((cotangent, v))
    frames = here * tm_count
    v_halo = from_neighbours(v[:, :1], v[:, rows - 1 :], 1)
    cot = to_rows(cotangent)
    cot_halo = from_neighbours(cot[:, :1], cot[:, rows - 1 :], 2)

    block = (v.shape, BF16)
    edge = ((frames, 1, channels, width), BF16)
    wide = ((frames, rows + 2, 3 * channels, width), BF16)

    inner, slope, first, last = call(
        pre_kernel, [block, (v.shape, F32), edge, edge], [wide], 0, v, *v_halo, forward_weight(kernel_a)
    )
    inner_halo = from_neighbours(first, last, 3)
    grad_pre, first, last = call(
        grad_pre_kernel, [block, edge, edge], [wide], 0, cot, *cot_halo, backward_weight(kernel_b), slope
    )
    grad_halo = from_neighbours(first, last, 4)
    video_rows, first, last = call(
        video_kernel, [block, edge, edge], [wide], 0, inner, *inner_halo, forward_weight(kernel_b), v
    )
    video_halo = from_neighbours(first, last, 5)
    video = to_frames(video_rows)
    (grad_rows,) = call(input_grad_kernel, [block], [wide], 0, grad_pre, *grad_halo, backward_weight(kernel_a), v, cot)
    input_grad = swap(grad_rows, 6).reshape(video_in.shape)

    column = jnp.arange(width, dtype=jnp.int32) // 2
    pool = (column[:, None] == jnp.arange(width // 2, dtype=jnp.int32)[None, :]).astype(BF16) * 0.25
    pool = jnp.concatenate([pool, pool], axis=0).astype(BF16)
    b, e, c, o = plane_kernel.shape
    plane_weight = plane_kernel.reshape(b * e * c, o).T
    time_weight = time_kernel.reshape(-1, time_kernel.shape[2]).T
    maps, time_scores = call(
        score_kernel,
        [((LISTED, rows, width), F32), ((rows // 2, 1, width // 2), F32)],
        [
            ((1, rows + 2, 3 * channels, width), BF16),
            (((frames + 2) * channels, width // 2), BF16),
        ],
        1,
        listed,
        video_rows,
        *video_halo,
        plane_weight,
        plane_head.astype(F32)[:, None],
        pool,
        time_weight,
        time_mixer.astype(F32).T,
        time_head.astype(F32)[:, None],
    )
    groups = tm_count // LISTED
    moved = swap(maps, 7)
    moved = moved.reshape(groups, tm_count * rows // groups, width)
    if groups > 1:
        mine = lax.rem(lax.axis_index("tm"), groups)
        moved = lax.dynamic_index_in_dim(moved, mine, 0, keepdims=True)
    plane_scores = moved[:, None]
    return (video, input_grad, plane_scores, time_scores.reshape(1, rows // 2, width // 2))


def solution(mesh):
    return jax.shard_map(
        shards,
        mesh=mesh,
        in_specs=(
            P("tm", "space", None, None),
            P("tm", "space", None, None),
            P(),
            P(),
            P(),
            P(),
            P(),
            P(),
            P(),
            P(),
        ),
        out_specs=(
            P("tm", "space", None, None),
            P("tm", "space", None, None),
            P("tm", "space", None, None),
            P("space", "tm", None),
        ),
        check_vma=False,
    )
```

```python
import functools

import jax
import jax.numpy as jnp
from jax import lax
from jax.experimental import pallas as pl
from jax.experimental.pallas import tpu as pltpu
from jax.sharding import PartitionSpec as P


LISTED = 8
F32 = jnp.float32
BF16 = jnp.bfloat16


def logistic(values):
    return 1.0 / (1.0 + jnp.exp(-values))


def slope_of(values):
    s = logistic(values)
    return s * (1.0 + values * (1.0 - s))


def store_shifted(wide_ref, t, row, values):
    channels, width = values.shape
    lane = lax.broadcasted_iota(jnp.int32, values.shape, 1)
    before = jnp.where(lane == 0, 0.0, pltpu.roll(values, 1, 1))
    after = jnp.where(lane == width - 1, 0.0, pltpu.roll(values, width - 1, 1))
    wide_ref[t, row, 0:channels] = before.astype(BF16)
    wide_ref[t, row, channels : 2 * channels] = values.astype(BF16)
    wide_ref[t, row, 2 * channels : 3 * channels] = after.astype(BF16)


def fill(wide_ref, main_ref, top_ref, bottom_ref, change):
    frames, rows = main_ref.shape[:2]

    def per_frame(t, _):
        store_shifted(wide_ref, t, 0, change(top_ref[t, 0].astype(F32)))
        store_shifted(wide_ref, t, rows + 1, change(bottom_ref[t, 0].astype(F32)))
        for row in range(rows):
            store_shifted(wide_ref, t, row + 1, change(main_ref[t, row].astype(F32)))
        return 0

    lax.fori_loop(0, frames, per_frame, 0)


def slab(wide_ref, t, row):
    depth = 3 * wide_ref.shape[2]
    width = wide_ref.shape[3]
    left = wide_ref[t, pl.ds(row, 3)].reshape(depth, width)
    right = wide_ref[t, pl.ds(row + 1, 3)].reshape(depth, width)
    return jnp.concatenate([left, right], axis=1)


def conv_loop(wide_ref, weight_ref, rows, emit):
    frames = wide_ref.shape[0]
    out = weight_ref.shape[0] // 3

    def product(t, row):
        return jnp.dot(weight_ref[...], slab(wide_ref, t, row), preferred_element_type=F32)

    def pair(i, _):
        row = 2 * i
        first = product(0, row)

        def step(t, carry):
            ready, early = carry
            z = product(t, row)
            emit(t - 1, row, ready + z[2 * out :])
            return early + z[out : 2 * out], z[:out]

        carry = (first[out : 2 * out], first[:out])
        if frames <= 8:
            for t in range(1, frames):
                carry = step(t, carry)
        else:
            carry = lax.fori_loop(1, frames, step, carry)
        emit(frames - 1, row, carry[0])
        return 0

    lax.fori_loop(0, rows // 2, pair, 0)


def each_row(emit_row, width):
    def emit(t, row, total):
        emit_row(t, row, total[:, :width])
        emit_row(t, row + 1, total[:, width:])

    return emit


def edges(out_ref, first_ref, last_ref):
    rows = out_ref.shape[1]
    first_ref[...] = out_ref[:, 0:1]
    last_ref[...] = out_ref[:, rows - 1 : rows]


def pre_kernel(main_ref, top_ref, bottom_ref, weight_ref, inner_ref, slope_ref, first_ref, last_ref, wide_ref):
    rows, width = main_ref.shape[1], main_ref.shape[3]
    fill(wide_ref, main_ref, top_ref, bottom_ref, lambda v: v * logistic(v))

    def emit(t, row, total):
        s = logistic(total)
        inner_ref[t, row] = (total * s).astype(BF16)
        slope_ref[t, row] = s * (1.0 + total * (1.0 - s))

    conv_loop(wide_ref, weight_ref, rows, each_row(emit, width))
    edges(inner_ref, first_ref, last_ref)


def grad_pre_kernel(main_ref, top_ref, bottom_ref, weight_ref, slope_ref, out_ref, first_ref, last_ref, wide_ref):
    rows, width = main_ref.shape[1], main_ref.shape[3]
    fill(wide_ref, main_ref, top_ref, bottom_ref, lambda v: v)

    def emit(t, row, total):
        out_ref[t, row] = (total * slope_ref[t, row]).astype(BF16)

    conv_loop(wide_ref, weight_ref, rows, each_row(emit, width))
    edges(out_ref, first_ref, last_ref)


def video_kernel(main_ref, top_ref, bottom_ref, weight_ref, in_ref, out_ref, first_ref, last_ref, wide_ref):
    rows, width = main_ref.shape[1], main_ref.shape[3]
    fill(wide_ref, main_ref, top_ref, bottom_ref, lambda v: v)

    def emit(t, row, total):
        out_ref[t, row] = (in_ref[t, row].astype(F32) + total).astype(BF16)

    conv_loop(wide_ref, weight_ref, rows, each_row(emit, width))
    edges(out_ref, first_ref, last_ref)


def input_grad_kernel(main_ref, top_ref, bottom_ref, weight_ref, in_ref, cot_ref, out_ref, wide_ref):
    rows, width = main_ref.shape[1], main_ref.shape[3]
    fill(wide_ref, main_ref, top_ref, bottom_ref, lambda v: v)

    def emit(t, row, total):
        gain = slope_of(in_ref[t, row].astype(F32))
        out_ref[t, row] = (cot_ref[t, row].astype(F32) + total * gain).astype(BF16)

    conv_loop(wide_ref, weight_ref, rows, each_row(emit, width))


def score_kernel(
    listed_ref,
    main_ref,
    top_ref,
    bottom_ref,
    plane_ref,
    plane_head_ref,
    pool_ref,
    time_ref,
    mixer_ref,
    time_head_ref,
    plane_out_ref,
    time_out_ref,
    wide_ref,
    pooled_ref,
):
    frames, rows, channels, width = main_ref.shape
    half = width // 2

    def per_listed(k, _):
        t = listed_ref[k]
        store_shifted(wide_ref, 0, 0, top_ref[t, 0].astype(F32))
        store_shifted(wide_ref, 0, rows + 1, bottom_ref[t, 0].astype(F32))
        for row in range(rows):
            store_shifted(wide_ref, 0, row + 1, main_ref[t, row].astype(F32))
        for row in range(0, rows, 2):
            g = jnp.dot(plane_ref[...], slab(wide_ref, 0, row), preferred_element_type=F32)
            scores = jnp.sum(g * logistic(g) * plane_head_ref[...], axis=0, keepdims=True)
            plane_out_ref[k, row : row + 1] = scores[:, :width]
            plane_out_ref[k, row + 1 : row + 2] = scores[:, width:]
        return 0

    lax.fori_loop(0, plane_out_ref.shape[0], per_listed, 0)

    def per_row(i, _):
        zero = jnp.zeros((channels, half), BF16)
        pooled_ref[0:channels] = zero
        pooled_ref[(frames + 1) * channels :] = zero
        for t in range(frames):
            both = jnp.concatenate([main_ref[t, 2 * i], main_ref[t, 2 * i + 1]], axis=1)
            mean = jnp.dot(both, pool_ref[...], preferred_element_type=F32)
            pooled_ref[(t + 1) * channels : (t + 2) * channels] = mean.astype(BF16)
        total = jnp.zeros((time_ref.shape[0], half), F32)
        for t in range(frames):
            q = jnp.dot(
                time_ref[...],
                pooled_ref[t * channels : (t + 3) * channels],
                preferred_element_type=F32,
            )
            total = total + q * logistic(q)
        mixed = jnp.dot(
            mixer_ref[...],
            total / frames,
            precision=lax.Precision.HIGHEST,
            preferred_element_type=F32,
        )
        time_out_ref[i] = jnp.sum(
            mixed * logistic(mixed) * time_head_ref[...], axis=0, keepdims=True
        )
        return 0

    lax.fori_loop(0, rows // 2, per_row, 0)


def call(kernel, outs, scratch, smem, *operands):
    return run(kernel, outs, scratch, smem, operands)


def run(kernel, outs, scratch, smem, operands):
    vmem = pl.BlockSpec(memory_space=pltpu.VMEM)
    specs = [pl.BlockSpec(memory_space=pltpu.SMEM)] * smem + [vmem] * (len(operands) - smem)
    return pl.pallas_call(
        kernel,
        out_shape=[jax.ShapeDtypeStruct(shape, dtype) for shape, dtype in outs],
        in_specs=specs,
        out_specs=[vmem] * len(outs),
        scratch_shapes=[pltpu.VMEM(shape, dtype) for shape, dtype in scratch],
        compiler_params=pltpu.CompilerParams(vmem_limit_bytes=56 * 1024 * 1024),
    )(*operands)


def forward_weight(kernel):
    a, b, e, c, o = kernel.shape
    return kernel.transpose(0, 4, 1, 2, 3).reshape(a * o, b * e * c)


def backward_weight(kernel):
    a, b, e, o, c = kernel.shape
    return kernel[::-1, ::-1, ::-1].transpose(0, 3, 1, 2, 4).reshape(a * o, b * e * c)


def halo_kernel(first_ref, last_ref, top_ref, bottom_ref, send_sem, recv_sem):
    parts, tiles = lax.axis_size("tm"), lax.axis_size("space")
    place = lax.axis_index("space") * parts + lax.axis_index("tm")
    has_before, has_after = place > 0, place < parts * tiles - 1
    lower, upper = jnp.maximum(place - 1, 0), jnp.minimum(place + 1, parts * tiles - 1)
    before = (lax.rem(lower, parts), lower // parts)
    after = (lax.rem(upper, parts), upper // parts)

    def move(source, target, slot, device):
        return pltpu.make_async_remote_copy(
            src_ref=source,
            dst_ref=target,
            send_sem=send_sem.at[slot],
            recv_sem=recv_sem.at[slot],
            device_id=device,
            device_id_type=pl.DeviceIdType.MESH,
        )

    def down():
        return move(first_ref, bottom_ref, 0, before)

    def up():
        return move(last_ref, top_ref, 1, after)

    barrier = pltpu.get_barrier_semaphore()

    @pl.when(has_before)
    def _():
        pl.semaphore_signal(barrier, inc=1, device_id=before, device_id_type=pl.DeviceIdType.MESH)

    @pl.when(has_after)
    def _():
        pl.semaphore_signal(barrier, inc=1, device_id=after, device_id_type=pl.DeviceIdType.MESH)

    pl.semaphore_wait(barrier, has_before.astype(jnp.int32) + has_after.astype(jnp.int32))

    @pl.when(has_before)
    def _():
        down().start()

    @pl.when(has_after)
    def _():
        up().start()

    @pl.when(jnp.logical_not(has_before))
    def _():
        top_ref[...] = jnp.zeros(top_ref.shape, top_ref.dtype)

    @pl.when(jnp.logical_not(has_after))
    def _():
        bottom_ref[...] = jnp.zeros(bottom_ref.shape, bottom_ref.dtype)

    @pl.when(has_before)
    def _():
        down().wait_send()
        up().wait_recv()

    @pl.when(has_after)
    def _():
        up().wait_send()
        down().wait_recv()


def from_neighbours(first, last, number):
    vmem = pl.BlockSpec(memory_space=pltpu.VMEM)
    edge = jax.ShapeDtypeStruct(first.shape, first.dtype)
    return pl.pallas_call(
        halo_kernel,
        name="halo",
        out_shape=[edge, edge],
        in_specs=[vmem] * 2,
        out_specs=[vmem] * 2,
        scratch_shapes=[pltpu.SemaphoreType.DMA((2,)), pltpu.SemaphoreType.DMA((2,))],
        compiler_params=pltpu.CompilerParams(collective_id=number, has_side_effects=True),
    )(first, last)


def swap_kernel(groups, *refs):
    count = len(groups)
    pairs = list(zip(groups, refs[:count], refs[count : 2 * count]))
    local_sem, send_sem, recv_sem = refs[2 * count :]
    parts = lax.axis_size("tm")
    me, tile = lax.axis_index("tm"), lax.axis_index("space")
    barrier = pltpu.get_barrier_semaphore()
    for d in range(1, parts):
        pl.semaphore_signal(
            barrier,
            inc=1,
            device_id=(lax.rem(me + d, parts), tile),
            device_id_type=pl.DeviceIdType.MESH,
        )
    pl.semaphore_wait(barrier, parts - 1)
    copies = []
    for n, (group, in_ref, out_ref) in enumerate(pairs):
        for d in range(1, parts):
            peer = lax.rem(me + d, parts)
            copies.append(
                pltpu.make_async_remote_copy(
                    src_ref=in_ref.at[peer // group],
                    dst_ref=out_ref.at[me],
                    send_sem=send_sem.at[n, d],
                    recv_sem=recv_sem.at[n, d],
                    device_id=(peer, tile),
                    device_id_type=pl.DeviceIdType.MESH,
                )
            )
    for n, (group, in_ref, out_ref) in enumerate(pairs):
        copies.append(pltpu.make_async_copy(in_ref.at[me // group], out_ref.at[me], local_sem.at[n]))
    for copy in copies:
        copy.start()
    for copy in copies:
        copy.wait()


def swap(number, *arrays):
    parts = lax.axis_size("tm")
    anywhere = pl.BlockSpec(memory_space=pl.ANY)
    count = len(arrays)
    return pl.pallas_call(
        functools.partial(swap_kernel, [parts // array.shape[0] for array in arrays]),
        name="swap",
        out_shape=[jax.ShapeDtypeStruct((parts,) + array.shape[1:], array.dtype) for array in arrays],
        in_specs=[anywhere] * count,
        out_specs=[anywhere] * count,
        scratch_shapes=[
            pltpu.SemaphoreType.DMA((count,)),
            pltpu.SemaphoreType.DMA((count, parts)),
            pltpu.SemaphoreType.DMA((count, parts)),
        ],
        compiler_params=pltpu.CompilerParams(collective_id=number, has_side_effects=True),
    )(*arrays)


def shards(
    video_in,
    cotangent,
    kernel_a,
    kernel_b,
    plane_kernel,
    plane_head,
    time_kernel,
    time_mixer,
    time_head,
    listed,
):
    to_rows = functools.partial(lax.all_to_all, axis_name="tm", split_axis=1, concat_axis=0, tiled=True)
    to_frames = functools.partial(lax.all_to_all, axis_name="tm", split_axis=0, concat_axis=1, tiled=True)
    tm_count = lax.axis_size("tm")

    here, height, channels, width = video_in.shape
    rows = height // tm_count
    (v,) = swap(0, video_in.reshape(tm_count, rows, channels, width))
    cotangent, v = lax.optimization_barrier((cotangent, v))
    frames = here * tm_count
    v_halo = from_neighbours(v[:, :1], v[:, rows - 1 :], 1)
    cot = to_rows(cotangent)
    cot_halo = from_neighbours(cot[:, :1], cot[:, rows - 1 :], 2)

    block = (v.shape, BF16)
    edge = ((frames, 1, channels, width), BF16)
    wide = ((frames, rows + 2, 3 * channels, width), BF16)

    inner, slope, first, last = call(
        pre_kernel, [block, (v.shape, F32), edge, edge], [wide], 0, v, *v_halo, forward_weight(kernel_a)
    )
    inner_halo = from_neighbours(first, last, 3)
    grad_pre, first, last = call(
        grad_pre_kernel, [block, edge, edge], [wide], 0, cot, *cot_halo, backward_weight(kernel_b), slope
    )
    grad_halo = from_neighbours(first, last, 4)
    video_rows, first, last = call(
        video_kernel, [block, edge, edge], [wide], 0, inner, *inner_halo, forward_weight(kernel_b), v
    )
    video_halo = from_neighbours(first, last, 5)
    video = to_frames(video_rows)
    (grad_rows,) = call(input_grad_kernel, [block], [wide], 0, grad_pre, *grad_halo, backward_weight(kernel_a), v, cot)

    column = jnp.arange(width, dtype=jnp.int32) // 2
    pool = (column[:, None] == jnp.arange(width // 2, dtype=jnp.int32)[None, :]).astype(BF16) * 0.25
    pool = jnp.concatenate([pool, pool], axis=0).astype(BF16)
    b, e, c, o = plane_kernel.shape
    plane_weight = plane_kernel.reshape(b * e * c, o).T
    time_weight = time_kernel.reshape(-1, time_kernel.shape[2]).T
    maps, time_scores = call(
        score_kernel,
        [((LISTED, rows, width), F32), ((rows // 2, 1, width // 2), F32)],
        [
            ((1, rows + 2, 3 * channels, width), BF16),
            (((frames + 2) * channels, width // 2), BF16),
        ],
        1,
        listed,
        video_rows,
        *video_halo,
        plane_weight,
        plane_head.astype(F32)[:, None],
        pool,
        time_weight,
        time_mixer.astype(F32).T,
        time_head.astype(F32)[:, None],
    )
    groups = tm_count // LISTED
    input_grad, moved = swap(6, grad_rows, maps)
    input_grad = input_grad.reshape(video_in.shape)
    moved = moved.reshape(groups, tm_count * rows // groups, width)
    if groups > 1:
        mine = lax.rem(lax.axis_index("tm"), groups)
        moved = lax.dynamic_index_in_dim(moved, mine, 0, keepdims=True)
    plane_scores = moved[:, None]
    return (video, input_grad, plane_scores, time_scores.reshape(1, rows // 2, width // 2))


def solution(mesh):
    return jax.shard_map(
        shards,
        mesh=mesh,
        in_specs=(
            P("tm", "space", None, None),
            P("tm", "space", None, None),
            P(),
            P(),
            P(),
            P(),
            P(),
            P(),
            P(),
            P(),
        ),
        out_specs=(
            P("tm", "space", None, None),
            P("tm", "space", None, None),
            P("tm", "space", None, None),
            P("space", "tm", None),
        ),
        check_vma=False,
    )
```
